32 devices in a mesh: tm: 16 (over z, y, x), space: 2 (over core).
Axes of the slice: x: 2, y: 2, z: 4, core: 2. Of those that a mesh axis runs over, the one named last changes fastest.
Arguments:
- source: float32 [64, 64, 512], P('tm', None, 'space'), may hold values from -3 to 3
- initial: float32 [64, 512], P(None, 'space'), may hold values from -6 to 6
- mass: float32 [64, 512], P(None, 'space'), may hold values from 0.8 to 1.25
- inverses: bfloat16 [3, 64, 64, 512], P(None, None, None, 'space'), may hold values from -0.3 to 1, as said below
- couplings: float32 [3, 6, 16, 16], replicated, may hold values from -0.375 to 0.375
- neighbours: int32 [6, 512], P(None, 'space'), may hold values from 0 to 288, as said below
- sends: int32 [2, 32], P(None, 'space'), may hold values from 0 to 255, as said below
Outputs:
- states: float32 [64, 64, 512], P('tm', None, 'space')
The draws below stay inside these ranges and needn't reach their ends.
Inputs may be any that keep to these rules, and one draw needn't show every extreme that they name: `neighbours`: each device's elements form a 16 x 4 x 4 block in its own order; an entry below 256 is a slot of the same device, 256 + j the j-th upper-face element of the device below, 272 + j the j-th lower-face element of the device above, 288 no neighbour. `sends`: row 0 lists the device's lower span-end elements, row 1 its upper ones, both in the same order of position on the face. `inverses`: each block is the identity scaled per node plus off-diagonal entries.
All inputs are finite; a program needn't handle non-finite values.
Results may differ from the reference program's by a relative error of at most 0.0003.
Values sent between devices are 32-bit elements; how exact they have to be, the bound alone decides.
A program may use at most 64 MiB of HBM per device.

```python
import math
import jax
import jax.numpy as jnp
from jax import lax

NODES = 64
TRACE = 16
LEVELS = 3
BX = 16
BY = 4
BZ = 4
E_DEV = 256
FACE = 16
ELEMS = 512
STEPS = 64
GROUPS = 4
N_TM = 16


def block_layout(key):
    blocks = ELEMS // E_DEV
    layout_keys = jax.random.split(jax.random.fold_in(key, 11), blocks)
    orders = jax.vmap(lambda one_key: jax.random.permutation(one_key, E_DEV))(layout_keys).astype(jnp.int32)
    placing = jnp.argsort(orders, axis=1).astype(jnp.int32)

    def one_block(order, place_of):
        cell = order
        along_x = cell % BX
        along_y = cell // BX % BY
        along_z = cell // (BX * BY)
        face_pos = along_y + BY * along_z
        blank = E_DEV + 2 * FACE

        def lookup(target):
            return place_of[jnp.clip(target, 0, E_DEV - 1)]
        face_lo_x = jnp.where(along_x > 0, lookup(cell - 1), E_DEV + face_pos)
        face_hi_x = jnp.where(along_x < BX - 1, lookup(cell + 1), E_DEV + FACE + face_pos)
        face_lo_y = jnp.where(along_y > 0, lookup(cell - BX), blank)
        face_hi_y = jnp.where(along_y < BY - 1, lookup(cell + BX), blank)
        face_lo_z = jnp.where(along_z > 0, lookup(cell - BX * BY), blank)
        face_hi_z = jnp.where(along_z < BZ - 1, lookup(cell + BX * BY), blank)
        linked = jnp.stack([face_lo_x, face_hi_x, face_lo_y, face_hi_y, face_lo_z, face_hi_z])
        face_ids = jnp.arange(FACE, dtype=jnp.int32)
        lower_list = place_of[BX * face_ids]
        upper_list = place_of[BX * face_ids + BX - 1]
        return (linked.astype(jnp.int32), jnp.stack([lower_list, upper_list]).astype(jnp.int32))
    linked_all, lists_all = jax.vmap(one_block)(orders, placing)
    return (linked_all, lists_all)


def draw_neighbours(key, part):
    linked_all, lists_all = block_layout(key)
    return jnp.transpose(linked_all, (1, 0, 2)).reshape(6, ELEMS)


def draw_sends(key, part):
    linked_all, lists_all = block_layout(key)
    return jnp.transpose(lists_all, (1, 0, 2)).reshape(2, FACE * (ELEMS // E_DEV))


def draw_inverses(key, part):
    key_diag, key_off = jax.random.split(jax.random.fold_in(key, 21), 2)
    diagonal = jax.random.uniform(key_diag, (LEVELS, NODES, ELEMS), jnp.float32, 0.5, 1.0)
    spread = jnp.clip(jax.random.normal(key_off, (LEVELS, NODES, NODES, ELEMS), jnp.float32), -6.0, 6.0) * (0.3 / 8.0)
    identity = jnp.eye(NODES, dtype=jnp.float32)[None, :, :, None]
    blocks = spread * (1.0 - identity) + identity * diagonal[:, :, None, :]
    return blocks.astype(jnp.bfloat16)


def level_of(own_key, extent, cuts, low, largest):
    loudness, own = 1.0, jax.random.fold_in(own_key, 6)
    for dim, parts in cuts:
        draws = jnp.exp(jax.random.uniform(jax.random.fold_in(own, dim), (parts,), jnp.float32, low / len(cuts), largest / len(cuts)))
        loudness = loudness * jnp.repeat(draws, extent[dim] // parts).reshape([-1 if axis == dim else 1 for axis in range(len(extent))])
    return loudness


def bell_draw(key, extent, width, bound, cuts=(), held_as=jnp.bfloat16):
    values = width * jax.random.normal(key, extent, jnp.float32)
    if cuts:
        values = values * level_of(key, extent, cuts, -0.22, 0.18)
    return jnp.clip(values, -bound, bound).astype(held_as)


def setup_inputs(seed: int = 0) -> dict:
    key_of = jax.random.split(jax.random.key(seed), 8)
    source = bell_draw(key_of[0], (STEPS, NODES, ELEMS), 0.5, 3.0, ((0, 16), (2, 2)), jnp.float32)
    initial = bell_draw(key_of[1], (NODES, ELEMS), 1.0, 6.0, ((1, 2),), jnp.float32)
    mass = jnp.clip(jnp.exp(math.log(1.25) - 0.4462871 * jax.random.uniform(key_of[2], (NODES, ELEMS), jnp.float32) ** level_of(key_of[2], (NODES, ELEMS), ((1, 2),), -0.2, 0.2)), 0.8, 1.25)
    inverses = draw_inverses(jax.random.fold_in(key_of[7], 71), 0)
    couplings = bell_draw(key_of[4], (LEVELS, 6, TRACE, TRACE), 0.06, 0.375, (), jnp.float32)
    neighbours = draw_neighbours(jax.random.fold_in(key_of[7], 71), 0)
    sends = draw_sends(jax.random.fold_in(key_of[7], 71), 0)
    return dict(source=source, initial=initial, mass=mass, inverses=inverses, couplings=couplings, neighbours=neighbours, sends=sends)


def trace_faces(state):
    elements = state.shape[-1]
    node_cube = state.reshape(state.shape[:-2] + (4, 4, 4, elements))
    face_sides = [node_cube[..., :, :, 0, :], node_cube[..., :, :, 3, :], node_cube[..., :, 0, :, :],
                  node_cube[..., :, 3, :, :], node_cube[..., 0, :, :, :], node_cube[..., 3, :, :, :]]
    return jnp.stack([one_side.reshape(state.shape[:-2] + (16, elements)) for one_side in face_sides], axis=-3)


def coupling_table(coupling):
    lifting = trace_faces(jnp.eye(64, dtype=coupling.dtype))
    return jnp.einsum("fkn,fkm->nfm", lifting, coupling, precision=lax.Precision.HIGHEST).reshape(64, 96)


def propagate(state, inverse, mass, table, neighbours, sends):
    batch = state.shape[0]
    blocks = ELEMS // E_DEV
    traces = trace_faces(state).reshape(batch, 6, 16, blocks, E_DEV)
    send_rows = sends.reshape(2, blocks, FACE)
    lower = jnp.take_along_axis(traces[:, 0], send_rows[0][None, None], axis=-1)
    upper = jnp.take_along_axis(traces[:, 1], send_rows[1][None, None], axis=-1)
    blank_block = jnp.zeros((batch, 16, 1, FACE), state.dtype)
    from_below = jnp.concatenate([blank_block, upper[:, :, :-1]], axis=2)
    from_above = jnp.concatenate([lower[:, :, 1:], blank_block], axis=2)
    blank_slot = jnp.zeros((batch, 16, blocks, 1), state.dtype)
    slots = neighbours.reshape(6, blocks, E_DEV)
    picked = []
    for face in range(6):
        extended = jnp.concatenate([traces[:, face ^ 1], from_below, from_above, blank_slot], axis=-1)
        picked.append(jnp.take_along_axis(extended, slots[face][None, None], axis=-1))
    stacked = jnp.stack(picked, axis=1).reshape(batch, 96, ELEMS)
    coupled = jnp.einsum("nk,bke->bne", table, stacked, precision=lax.Precision.HIGHEST)
    rhs_local = mass[None] * state - coupled
    return jnp.einsum("ije,bje->bie", inverse.astype(jnp.float32), rhs_local, precision=lax.Precision.HIGHEST)


def reference(source, initial, mass, inverses, couplings, neighbours, sends):
    tables = [coupling_table(couplings[level_index]) for level_index in range(3)]

    def advance_level(state, level_index):
        return propagate(state, inverses[level_index], mass, tables[level_index], neighbours, sends)

    sources = source.reshape(N_TM, 4, 64, ELEMS)
    device = jnp.arange(N_TM)[:, None, None]
    fine_state = jnp.zeros((N_TM, 64, ELEMS), jnp.float32)
    for offset in range(1, 4):
        fine_state = advance_level(fine_state, 0) + sources[:, offset]
    carried = advance_level(fine_state, 0)
    arrived = jnp.concatenate([jnp.zeros((1, 64, ELEMS), jnp.float32), carried[:-1]], axis=0)
    residual = jnp.where(device == 0, initial[None], sources[:, 0] + arrived)
    grouped = residual.reshape(GROUPS, 4, 64, ELEMS)
    level_one = grouped[:, 1]
    for offset in range(2, 4):
        level_one = advance_level(level_one, 1) + grouped[:, offset]
    carried_one = advance_level(level_one, 1)
    coarse_rhs = grouped[:, 0] + jnp.concatenate([jnp.zeros((1, 64, ELEMS), jnp.float32), carried_one[:-1]], axis=0)
    coarse_value = coarse_rhs[0:1]
    coarse_list = [coarse_value]
    for group_index in range(1, GROUPS):
        coarse_value = advance_level(coarse_value, 2) + coarse_rhs[group_index:group_index + 1]
        coarse_list.append(coarse_value)
    corrected = jnp.concatenate(coarse_list, axis=0)
    level_values = [corrected]
    for offset in range(1, 4):
        corrected = advance_level(corrected, 1) + grouped[:, offset]
        level_values.append(corrected)
    current = jnp.stack(level_values, axis=1).reshape(N_TM, 64, ELEMS)
    states = [current]
    for offset in range(1, 4):
        current = advance_level(current, 0) + sources[:, offset]
        states.append(current)
    return jnp.stack(states, axis=1).reshape(STEPS, 64, ELEMS)
```

```python
import functools
import jax
import jax.numpy as jnp
from jax import lax
from jax.experimental import pallas as pl
from jax.experimental.pallas import tpu as pltpu
from jax.sharding import PartitionSpec as P

MESH = pl.DeviceIdType.MESH
HI = lax.Precision.HIGHEST


def lane_take(block, index):
    return jnp.take_along_axis(block, index, axis=1, mode="promise_in_bounds")


def kernel(tm_size, space_size, source, initial, mass, inverses, couplings, neighbours, sends,
           out, inv, tables, state, traces, halo, rhs, low, high, slots, picks, where_halo,
           next_source, r_all, w_in, w_out,
           inv_sem, halo_send, halo_recv, slot_send, slot_recv, src_send, src_recv,
           r_send, r_recv, w_send, w_recv):
    f32 = jnp.float32
    d = lax.axis_index("tm")
    k = lax.axis_index("space")
    j = lax.rem(d, 4)
    m = lax.div(d, 4)
    groups = tm_size // 4
    above = lax.rem(k + 1, space_size)
    below = lax.rem(k + space_size - 1, space_size)
    peers = [4 * m + lax.rem(j + step, 4) for step in (1, 2, 3)]

    loads = [pltpu.make_async_copy(inverses.at[l], inv.at[l], inv_sem.at[l]) for l in range(3)]
    loads[0].start()
    loads[1].start()
    loads[2].start()

    barrier = pltpu.get_barrier_semaphore()

    def greet(t, s):
        pl.semaphore_signal(barrier, inc=1, device_id=(t, s), device_id_type=MESH)

    greet(d, above)
    greet(d, below)
    for peer in peers:
        greet(peer, k)

    @pl.when(d > 0)
    def _():
        greet(d - 1, k)

    @pl.when(d < tm_size - 1)
    def _():
        greet(d + 1, k)

    @pl.when(m > 0)
    def _():
        greet(d - 4, k)

    @pl.when(m < groups - 1)
    def _():
        greet(d + 4, k)

    slots[0] = jnp.zeros((8, 128), jnp.int32)
    slots[0, 0:2, 0:16] = sends[...]

    n = lax.broadcasted_iota(jnp.int32, (64, 96), 0)
    col = lax.broadcasted_iota(jnp.int32, (64, 96), 1)
    a, b, c = n & 3, (n >> 2) & 3, n >> 4
    face, point = col >> 4, col & 15
    axis = face >> 1
    fixed = jnp.where(axis == 0, a, jnp.where(axis == 1, b, c))
    place = jnp.where(axis == 0, b + 4 * c, jnp.where(axis == 1, a + 4 * c, a + 4 * b))
    lift = ((fixed == 3 * (face & 1)) & (place == point)).astype(f32)
    spread = (lax.broadcasted_iota(jnp.int32, (16, 96), 0)
              == (lax.broadcasted_iota(jnp.int32, (16, 96), 1) & 15)).astype(f32)
    same = (lax.broadcasted_iota(jnp.int32, (96, 96), 0) >> 4
            == lax.broadcasted_iota(jnp.int32, (96, 96), 1) >> 4)
    for l in range(3):
        wide = jnp.dot(couplings[l], spread, precision=HI, preferred_element_type=f32)
        tables[l] = jnp.dot(lift, jnp.where(same, wide, 0.0), precision=HI,
                            preferred_element_type=f32)

    nb = neighbours[...]
    picks[...] = jnp.where(nb < 256, nb, 512)

    pl.semaphore_wait(
        barrier,
        5 + (d > 0).astype(jnp.int32) + (d < tm_size - 1).astype(jnp.int32)
        + (m > 0).astype(jnp.int32) + (m < groups - 1).astype(jnp.int32))

    lists = [
        pltpu.make_async_remote_copy(slots.at[0], slots.at[1], slot_send.at[0], slot_recv.at[0],
                                     device_id=(d, above), device_id_type=MESH),
        pltpu.make_async_remote_copy(slots.at[0], slots.at[2], slot_send.at[1], slot_recv.at[1],
                                     device_id=(d, below), device_id_type=MESH)]
    for copy in lists:
        copy.start()

    back = jnp.maximum(d - 1, 0)
    forth = jnp.where(d > 0, d - 1, 1)
    ahead = pltpu.make_async_remote_copy(source.at[0], next_source, src_send, src_recv,
                                         device_id=(forth, k), device_id_type=MESH)

    @pl.when(d > 0)
    def _():
        ahead.start()

    @pl.when(d == tm_size - 1)
    def _():
        next_source[...] = jnp.zeros_like(next_source)

    for copy in lists:
        copy.wait()
    for row, (held, line, begin, exists) in enumerate(
            [(1, 1, 256, k > 0), (2, 0, 272, k < space_size - 1)]):
        for tile in (0, 1):
            lanes = pl.ds(128 * tile, 128)
            entry = jnp.broadcast_to(neighbours[row:row + 1, lanes], (8, 128)) - begin
            listed = jnp.broadcast_to(slots[held, line:line + 1, :], (8, 128))
            taken = lane_take(listed, jnp.clip(entry, 0, 15))
            limit = jnp.where(exists, 16, 0)
            valid = (entry >= 0) & (entry < limit)
            where_halo[row, :, lanes] = jnp.where(valid, taken, 512)

    def take_from(block, index_of):
        halves = []
        for tile in (0, 1):
            index = index_of(tile)
            spot = index & 127
            part = index >> 7
            halves.append(jnp.where(part == 0, lane_take(block[:, :128], spot),
                                    jnp.where(part == 1, lane_take(block[:, 128:], spot), 0.0)))
        return jnp.concatenate(halves, axis=1)

    def across(ref, begin, size, stride=None):
        return jnp.concatenate([ref[tile, pl.ds(begin, size, stride), :] for tile in (0, 1)], axis=1)

    def phi(level, slot, value):
        for tile in (0, 1):
            state[tile] = value[:, 128 * tile:128 * tile + 128]
        traces[slot, 0] = across(state, 0, 16, 4)
        traces[slot, 1] = across(state, 3, 16, 4)
        moves = [
            pltpu.make_async_remote_copy(traces.at[slot, 1], halo.at[slot, 0], halo_send.at[slot, 0],
                                         halo_recv.at[slot, 0], device_id=(d, above),
                                         device_id_type=MESH),
            pltpu.make_async_remote_copy(traces.at[slot, 0], halo.at[slot, 1], halo_send.at[slot, 1],
                                         halo_recv.at[slot, 1], device_id=(d, below),
                                         device_id_type=MESH)]
        for move in moves:
            move.start()
        faces = [
            traces[slot, 0], traces[slot, 1],
            jnp.concatenate([value[16 * q:16 * q + 4, :] for q in range(4)], axis=0),
            jnp.concatenate([value[16 * q + 12:16 * q + 16, :] for q in range(4)], axis=0),
            value[0:16, :], value[48:64, :]]
        picked = jnp.concatenate(
            [take_from(faces[f ^ 1], lambda tile, f=f: jnp.broadcast_to(
                picks[f:f + 1, 128 * tile:128 * tile + 128], (16, 128))) for f in range(6)], axis=0)
        coupled = jnp.dot(tables[level], picked, precision=HI, preferred_element_type=f32)
        known = mass[...] * value - coupled
        for tile in (0, 1):
            rhs[tile] = known[:, 128 * tile:128 * tile + 128]

        def early(q, total):
            for step in (1, 2):
                at = 4 * q + step
                total = total + inv[level, at].astype(f32) * across(rhs, at, 1)
            return total

        total = lax.fori_loop(0, 16, early, jnp.zeros((64, 256), f32), unroll=2)
        for move in moves:
            move.wait()
        for row, kept, first in ((0, low, 0), (1, high, 3)):
            got = take_from(halo[slot, row], lambda tile, row=row: jnp.concatenate(
                [where_halo[row, :, 128 * tile:128 * tile + 128]] * 2, axis=0))
            change = jnp.dot(couplings[level, 16 * row:16 * row + 16, :], got, precision=HI,
                             preferred_element_type=f32)
            kept[...] = across(rhs, first, 16, 4) - change

        def late(q, total):
            total = total + inv[level, 4 * q].astype(f32) * low[pl.ds(q, 1), :]
            return total + inv[level, 4 * q + 3].astype(f32) * high[pl.ds(q, 1), :]

        return lax.fori_loop(0, 16, late, total, unroll=2)

    loads[0].wait()
    value = source[1]
    value = phi(0, 0, value) + source[2]
    value = phi(0, 1, value) + source[3]
    value = phi(0, 0, value)

    @pl.when(d < tm_size - 1)
    def _():
        ahead.wait_recv()

    @pl.when(d > 0)
    def _():
        ahead.wait_send()

    r_all[j] = value + next_source[...]
    shares = [pltpu.make_async_remote_copy(r_all.at[j], r_all.at[j], r_send.at[i], r_recv.at[j],
                                           device_id=(peer, k), device_id_type=MESH)
              for i, peer in enumerate(peers)]
    for share in shares:
        share.start()

    def share_arrived(i):
        @pl.when(j != i)
        def _():
            pltpu.make_async_remote_copy(r_all.at[i], r_all.at[i], r_send.at[0], r_recv.at[i],
                                         device_id=(peers[0], k), device_id_type=MESH).wait_recv()

    loads[2].wait()
    first = phi(2, 1, initial[...])
    loads[1].wait()
    share_arrived(0)
    value = phi(1, 0, r_all[0])
    share_arrived(1)
    value = phi(1, 1, value + r_all[1])
    share_arrived(2)
    value = phi(1, 0, value + r_all[2])
    share_arrived(3)
    w_out[...] = value + r_all[3]
    for share in shares:
        share.wait_send()

    onward = pltpu.make_async_remote_copy(w_out, w_in, w_send, w_recv,
                                          device_id=(jnp.where(m < groups - 1, d + 4, d - 4), k),
                                          device_id_type=MESH)

    @pl.when(m == 0)
    def _():
        w_in[...] = initial[...]
        w_out[...] = w_out[...] + first

    @pl.when(m > 0)
    def _():
        onward.wait_recv()

    @pl.when((m > 0) & (m < groups - 1))
    def _():
        w_out[...] = w_out[...] + phi(2, 2, w_in[...])

    @pl.when(m < groups - 1)
    def _():
        onward.start()

    value = w_in[...]
    for i in (1, 2, 3):
        moved = phi(1, i % 2, value) + r_all[i - 1]
        value = jnp.where(j >= i, moved, value)
    out[0] = value
    for i in (1, 2, 3):
        value = phi(0, (i + 1) % 2, value) + source[i]
        out[i] = value

    @pl.when(m < groups - 1)
    def _():
        onward.wait_send()


def local(tm_size, space_size, source, initial, mass, inverses, couplings, neighbours, sends):
    f32 = jnp.float32
    turned = jnp.swapaxes(inverses, 1, 2)
    vmem = pl.BlockSpec(memory_space=pltpu.VMEM)
    dma = pltpu.SemaphoreType.DMA
    return pl.pallas_call(
        functools.partial(kernel, tm_size, space_size),
        out_shape=jax.ShapeDtypeStruct(source.shape, f32),
        in_specs=[vmem, vmem, vmem, pl.BlockSpec(memory_space=pl.ANY), vmem, vmem, vmem],
        out_specs=vmem,
        scratch_shapes=[
            pltpu.VMEM(turned.shape, jnp.bfloat16),
            pltpu.VMEM((3, 64, 96), f32),
            pltpu.VMEM((2, 64, 128), f32),
            pltpu.VMEM((3, 2, 16, 256), f32),
            pltpu.VMEM((3, 2, 16, 256), f32),
            pltpu.VMEM((2, 64, 128), f32),
            pltpu.VMEM((16, 256), f32),
            pltpu.VMEM((16, 256), f32),
            pltpu.VMEM((3, 8, 128), jnp.int32),
            pltpu.VMEM((6, 256), jnp.int32),
            pltpu.VMEM((2, 8, 256), jnp.int32),
            pltpu.VMEM((64, 256), f32),
            pltpu.VMEM((4, 64, 256), f32),
            pltpu.VMEM((64, 256), f32),
            pltpu.VMEM((64, 256), f32),
            dma((3,)), dma((3, 2)), dma((3, 2)), dma((2,)), dma((2,)), dma, dma,
            dma((3,)), dma((4,)), dma, dma,
        ],
        compiler_params=pltpu.CompilerParams(collective_id=0, has_side_effects=True),
        name="cycle",
    )(source, initial, mass, turned, couplings.reshape(3, 96, 16), neighbours, sends)


def solution(mesh):
    placed = (
        P("tm", None, "space"),
        P(None, "space"),
        P(None, "space"),
        P(None, None, None, "space"),
        P(),
        P(None, "space"),
        P(None, "space"),
    )
    return jax.shard_map(
        functools.partial(local, mesh.shape["tm"], mesh.shape["space"]),
        mesh=mesh, in_specs=placed, out_specs=P("tm", None, "space"), check_vma=False)
```

```python
import functools
import jax
import jax.numpy as jnp
from jax import lax
from jax.experimental import pallas as pl
from jax.experimental.pallas import tpu as pltpu
from jax.sharding import PartitionSpec as P

MESH = pl.DeviceIdType.MESH
HI = lax.Precision.HIGHEST


def lane_take(block, index):
    return jnp.take_along_axis(block, index, axis=1, mode="promise_in_bounds")


def kernel(tm_size, space_size, source, initial, mass, inverses, couplings, neighbours, sends,
           out, packed, stage, inv, tables, state, traces, halo, rhs, low, high, slots, picks, where_halo,
           next_source, r_all, w_in, w_out,
           inv_sem, halo_send, halo_recv, slot_send, slot_recv, src_send, src_recv,
           r_send, r_recv, w_send, w_recv):
    f32 = jnp.float32
    d = lax.axis_index("tm")
    k = lax.axis_index("space")
    j = lax.rem(d, 4)
    m = lax.div(d, 4)
    groups = tm_size // 4
    above = lax.rem(k + 1, space_size)
    below = lax.rem(k + space_size - 1, space_size)
    peers = [4 * m + lax.rem(j + step, 4) for step in (1, 2, 3)]

    loads = [pltpu.make_async_copy(inverses.at[l], packed.at[l], inv_sem.at[l]) for l in range(3)]
    loads[0].start()
    loads[1].start()
    loads[2].start()

    barrier = pltpu.get_barrier_semaphore()

    def greet(t, s):
        pl.semaphore_signal(barrier, inc=1, device_id=(t, s), device_id_type=MESH)

    greet(d, above)
    greet(d, below)
    for peer in peers:
        greet(peer, k)

    @pl.when(d > 0)
    def _():
        greet(d - 1, k)

    @pl.when(d < tm_size - 1)
    def _():
        greet(d + 1, k)

    @pl.when(m > 0)
    def _():
        greet(d - 4, k)

    @pl.when(m < groups - 1)
    def _():
        greet(d + 4, k)

    slots[0] = jnp.zeros((8, 128), jnp.int32)
    slots[0, 0:2, 0:16] = sends[...]

    n = lax.broadcasted_iota(jnp.int32, (64, 96), 0)
    col = lax.broadcasted_iota(jnp.int32, (64, 96), 1)
    a, b, c = n & 3, (n >> 2) & 3, n >> 4
    face, point = col >> 4, col & 15
    axis = face >> 1
    fixed = jnp.where(axis == 0, a, jnp.where(axis == 1, b, c))
    place = jnp.where(axis == 0, b + 4 * c, jnp.where(axis == 1, a + 4 * c, a + 4 * b))
    lift = ((fixed == 3 * (face & 1)) & (place == point)).astype(f32)
    spread = (lax.broadcasted_iota(jnp.int32, (16, 96), 0)
              == (lax.broadcasted_iota(jnp.int32, (16, 96), 1) & 15)).astype(f32)
    same = (lax.broadcasted_iota(jnp.int32, (96, 96), 0) >> 4
            == lax.broadcasted_iota(jnp.int32, (96, 96), 1) >> 4)
    for l in range(3):
        wide = jnp.dot(couplings[l], spread, precision=HI, preferred_element_type=f32)
        tables[l] = jnp.dot(lift, jnp.where(same, wide, 0.0), precision=HI,
                            preferred_element_type=f32)

    def prepare(level, begin, end):
        def block(part, carry):
            for i in range(8):
                whole = packed[level, 8 * part + i].astype(f32)
                for tile in (0, 1):
                    stage[tile, 64 * i:64 * i + 64, :] = whole[:, 128 * tile:128 * tile + 128]
            rows = pl.ds(pl.multiple_of(8 * part, 8), 8)
            for at in range(64):
                for tile in (0, 1):
                    inv[level, at, tile, rows, :] = stage[tile, pl.ds(at, 8, 64), :]
            return carry

        lax.fori_loop(begin, end, block, 0)

    nb = neighbours[...]
    picks[...] = jnp.where(nb < 256, nb, 512)

    loads[0].wait()
    prepare(0, 0, 8)
    loads[1].wait()
    loads[2].wait()

    pl.semaphore_wait(
        barrier,
        5 + (d > 0).astype(jnp.int32) + (d < tm_size - 1).astype(jnp.int32)
        + (m > 0).astype(jnp.int32) + (m < groups - 1).astype(jnp.int32))

    lists = [
        pltpu.make_async_remote_copy(slots.at[0], slots.at[1], slot_send.at[0], slot_recv.at[0],
                                     device_id=(d, above), device_id_type=MESH),
        pltpu.make_async_remote_copy(slots.at[0], slots.at[2], slot_send.at[1], slot_recv.at[1],
                                     device_id=(d, below), device_id_type=MESH)]
    for copy in lists:
        copy.start()

    back = jnp.maximum(d - 1, 0)
    forth = jnp.where(d > 0, d - 1, 1)
    ahead = pltpu.make_async_remote_copy(source.at[0], next_source, src_send, src_recv,
                                         device_id=(forth, k), device_id_type=MESH)

    @pl.when(d > 0)
    def _():
        ahead.start()

    @pl.when(d == tm_size - 1)
    def _():
        next_source[...] = jnp.zeros_like(next_source)

    for copy in lists:
        copy.wait()
    for row, (held, line, begin, exists) in enumerate(
            [(1, 1, 256, k > 0), (2, 0, 272, k < space_size - 1)]):
        for tile in (0, 1):
            lanes = pl.ds(128 * tile, 128)
            entry = jnp.broadcast_to(neighbours[row:row + 1, lanes], (8, 128)) - begin
            listed = jnp.broadcast_to(slots[held, line:line + 1, :], (8, 128))
            taken = lane_take(listed, jnp.clip(entry, 0, 15))
            limit = jnp.where(exists, 16, 0)
            valid = (entry >= 0) & (entry < limit)
            where_halo[row, :, lanes] = jnp.where(valid, taken, 512)

    def take_from(block, index_of):
        halves = []
        for tile in (0, 1):
            index = index_of(tile)
            spot = index & 127
            part = index >> 7
            halves.append(jnp.where(part == 0, lane_take(block[:, :128], spot),
                                    jnp.where(part == 1, lane_take(block[:, 128:], spot), 0.0)))
        return jnp.concatenate(halves, axis=1)

    def across(ref, begin, size, stride=None):
        return jnp.concatenate([ref[tile, pl.ds(begin, size, stride), :] for tile in (0, 1)], axis=1)

    def phi(level, slot, value, meanwhile=None):
        for tile in (0, 1):
            state[tile] = value[:, 128 * tile:128 * tile + 128]
        traces[slot, 0] = across(state, 0, 16, 4)
        traces[slot, 1] = across(state, 3, 16, 4)
        moves = [
            pltpu.make_async_remote_copy(traces.at[slot, 1], halo.at[slot, 0], halo_send.at[slot, 0],
                                         halo_recv.at[slot, 0], device_id=(d, above),
                                         device_id_type=MESH),
            pltpu.make_async_remote_copy(traces.at[slot, 0], halo.at[slot, 1], halo_send.at[slot, 1],
                                         halo_recv.at[slot, 1], device_id=(d, below),
                                         device_id_type=MESH)]
        for move in moves:
            move.start()
        faces = [
            traces[slot, 0], traces[slot, 1],
            jnp.concatenate([value[16 * q:16 * q + 4, :] for q in range(4)], axis=0),
            jnp.concatenate([value[16 * q + 12:16 * q + 16, :] for q in range(4)], axis=0),
            value[0:16, :], value[48:64, :]]
        picked = jnp.concatenate(
            [take_from(faces[f ^ 1], lambda tile, f=f: jnp.broadcast_to(
                picks[f:f + 1, 128 * tile:128 * tile + 128], (16, 128))) for f in range(6)], axis=0)
        coupled = jnp.dot(tables[level], picked, precision=HI, preferred_element_type=f32)
        known = mass[...] * value - coupled
        for tile in (0, 1):
            rhs[tile] = known[:, 128 * tile:128 * tile + 128]

        def early(q, total):
            for step in (1, 2):
                at = 4 * q + step
                total = total + inv[level, at] * rhs[:, pl.ds(at, 1), :]
            return total

        total = lax.fori_loop(0, 16, early, jnp.zeros((2, 64, 128), f32), unroll=2)
        if meanwhile is not None:
            prepare(*meanwhile)
        for move in moves:
            move.wait()
        for row, kept, first in ((0, low, 0), (1, high, 3)):
            got = take_from(halo[slot, row], lambda tile, row=row: jnp.concatenate(
                [where_halo[row, :, 128 * tile:128 * tile + 128]] * 2, axis=0))
            change = jnp.dot(couplings[level, 16 * row:16 * row + 16, :], got, precision=HI,
                             preferred_element_type=f32)
            for tile in (0, 1):
                kept[tile] = rhs[tile, pl.ds(first, 16, 4), :] - change[:, 128 * tile:128 * tile + 128]

        def late(q, total):
            total = total + inv[level, 4 * q] * low[:, pl.ds(q, 1), :]
            return total + inv[level, 4 * q + 3] * high[:, pl.ds(q, 1), :]

        total = lax.fori_loop(0, 16, late, total, unroll=2)
        return jnp.concatenate([total[0], total[1]], axis=1)

    value = source[1]
    value = phi(0, 0, value, (1, 0, 3)) + source[2]
    value = phi(0, 1, value, (1, 3, 6)) + source[3]
    value = phi(0, 0, value, (1, 6, 8))

    @pl.when(d < tm_size - 1)
    def _():
        ahead.wait_recv()

    @pl.when(d > 0)
    def _():
        ahead.wait_send()

    r_all[j] = value + next_source[...]
    shares = [pltpu.make_async_remote_copy(r_all.at[j], r_all.at[j], r_send.at[i], r_recv.at[j],
                                           device_id=(peer, k), device_id_type=MESH)
              for i, peer in enumerate(peers)]
    for share in shares:
        share.start()

    def share_arrived(i):
        @pl.when(j != i)
        def _():
            pltpu.make_async_remote_copy(r_all.at[i], r_all.at[i], r_send.at[0], r_recv.at[i],
                                         device_id=(peers[0], k), device_id_type=MESH).wait_recv()

    prepare(2, 0, 8)
    first = phi(2, 1, initial[...])
    share_arrived(0)
    value = phi(1, 0, r_all[0])
    share_arrived(1)
    value = phi(1, 1, value + r_all[1])
    share_arrived(2)
    value = phi(1, 0, value + r_all[2])
    share_arrived(3)
    w_out[...] = value + r_all[3]
    for share in shares:
        share.wait_send()

    onward = pltpu.make_async_remote_copy(w_out, w_in, w_send, w_recv,
                                          device_id=(jnp.where(m < groups - 1, d + 4, d - 4), k),
                                          device_id_type=MESH)

    @pl.when(m == 0)
    def _():
        w_in[...] = initial[...]
        w_out[...] = w_out[...] + first

    @pl.when(m > 0)
    def _():
        onward.wait_recv()

    @pl.when((m > 0) & (m < groups - 1))
    def _():
        w_out[...] = w_out[...] + phi(2, 2, w_in[...])

    @pl.when(m < groups - 1)
    def _():
        onward.start()

    value = w_in[...]
    for i in (1, 2, 3):
        moved = phi(1, i % 2, value) + r_all[i - 1]
        value = jnp.where(j >= i, moved, value)
    out[0] = value
    for i in (1, 2, 3):
        value = phi(0, (i + 1) % 2, value) + source[i]
        out[i] = value

    @pl.when(m < groups - 1)
    def _():
        onward.wait_send()


def local(tm_size, space_size, source, initial, mass, inverses, couplings, neighbours, sends):
    f32 = jnp.float32
    vmem = pl.BlockSpec(memory_space=pltpu.VMEM)
    dma = pltpu.SemaphoreType.DMA
    return pl.pallas_call(
        functools.partial(kernel, tm_size, space_size),
        out_shape=jax.ShapeDtypeStruct(source.shape, f32),
        in_specs=[vmem, vmem, vmem, pl.BlockSpec(memory_space=pl.ANY), vmem, vmem, vmem],
        out_specs=vmem,
        scratch_shapes=[
            pltpu.VMEM(inverses.shape, jnp.bfloat16),
            pltpu.VMEM((2, 512, 128), f32),
            pltpu.VMEM((3, 64, 2, 64, 128), f32),
            pltpu.VMEM((3, 64, 96), f32),
            pltpu.VMEM((2, 64, 128), f32),
            pltpu.VMEM((3, 2, 16, 256), f32),
            pltpu.VMEM((3, 2, 16, 256), f32),
            pltpu.VMEM((2, 64, 128), f32),
            pltpu.VMEM((2, 16, 128), f32),
            pltpu.VMEM((2, 16, 128), f32),
            pltpu.VMEM((3, 8, 128), jnp.int32),
            pltpu.VMEM((6, 256), jnp.int32),
            pltpu.VMEM((2, 8, 256), jnp.int32),
            pltpu.VMEM((64, 256), f32),
            pltpu.VMEM((4, 64, 256), f32),
            pltpu.VMEM((64, 256), f32),
            pltpu.VMEM((64, 256), f32),
            dma((3,)), dma((3, 2)), dma((3, 2)), dma((2,)), dma((2,)), dma, dma,
            dma((3,)), dma((4,)), dma, dma,
        ],
        compiler_params=pltpu.CompilerParams(collective_id=0, has_side_effects=True),
        name="cycle",
    )(source, initial, mass, inverses, couplings.reshape(3, 96, 16), neighbours, sends)


def solution(mesh):
    placed = (
        P("tm", None, "space"),
        P(None, "space"),
        P(None, "space"),
        P(None, None, None, "space"),
        P(),
        P(None, "space"),
        P(None, "space"),
    )
    return jax.shard_map(
        functools.partial(local, mesh.shape["tm"], mesh.shape["space"]),
        mesh=mesh, in_specs=placed, out_specs=P("tm", None, "space"), check_vma=False)
```

```python
import functools
import jax
import jax.numpy as jnp
from jax import lax
from jax.experimental import pallas as pl
from jax.experimental.pallas import tpu as pltpu
from jax.sharding import PartitionSpec as P

MESH = pl.DeviceIdType.MESH
HI = lax.Precision.HIGHEST


def lane_take(block, index):
    return jnp.take_along_axis(block, index, axis=1, mode="promise_in_bounds")


def kernel(tm_size, space_size, source, initial, mass, inverses, couplings, neighbours, sends,
           out, packed, stage, inv, tables, edges, state, traces, halo, rhs, low, high, slots, picks, where_halo,
           next_source, r_all, w_in, w_out,
           inv_sem, halo_send, halo_recv, slot_send, slot_recv, src_send, src_recv,
           r_send, r_recv, w_send, w_recv):
    f32 = jnp.float32
    d = lax.axis_index("tm")
    k = lax.axis_index("space")
    j = lax.rem(d, 4)
    m = lax.div(d, 4)
    groups = tm_size // 4
    above = lax.rem(k + 1, space_size)
    below = lax.rem(k + space_size - 1, space_size)
    peers = [4 * m + lax.rem(j + step, 4) for step in (1, 2, 3)]

    loads = [pltpu.make_async_copy(inverses.at[l], packed.at[l], inv_sem.at[l]) for l in range(3)]
    loads[0].start()
    loads[1].start()
    loads[2].start()

    barrier = pltpu.get_barrier_semaphore()

    def greet(t, s):
        pl.semaphore_signal(barrier, inc=1, device_id=(t, s), device_id_type=MESH)

    greet(d, above)
    greet(d, below)
    for peer in peers:
        greet(peer, k)

    @pl.when(d > 0)
    def _():
        greet(d - 1, k)

    @pl.when(d < tm_size - 1)
    def _():
        greet(d + 1, k)

    @pl.when(m > 0)
    def _():
        greet(d - 4, k)

    @pl.when(m < groups - 1)
    def _():
        greet(d + 4, k)

    slots[0] = jnp.zeros((8, 128), jnp.int32)
    slots[0, 0:2, 0:16] = sends[...]

    n = lax.broadcasted_iota(jnp.int32, (64, 96), 0)
    col = lax.broadcasted_iota(jnp.int32, (64, 96), 1)
    a, b, c = n & 3, (n >> 2) & 3, n >> 4
    face, point = col >> 4, col & 15
    axis = face >> 1
    fixed = jnp.where(axis == 0, a, jnp.where(axis == 1, b, c))
    place = jnp.where(axis == 0, b + 4 * c, jnp.where(axis == 1, a + 4 * c, a + 4 * b))
    lift = ((fixed == 3 * (face & 1)) & (place == point)).astype(f32)
    spread = (lax.broadcasted_iota(jnp.int32, (16, 96), 0)
              == (lax.broadcasted_iota(jnp.int32, (16, 96), 1) & 15)).astype(f32)
    same = (lax.broadcasted_iota(jnp.int32, (96, 96), 0) >> 4
            == lax.broadcasted_iota(jnp.int32, (96, 96), 1) >> 4)
    def split(x):
        top = x.astype(jnp.bfloat16)
        return top, (x - top.astype(f32)).astype(jnp.bfloat16)

    def stacked(x):
        top, rest = split(x)
        return jnp.concatenate([jnp.concatenate([top, top], axis=1),
                                jnp.concatenate([rest, rest], axis=1)], axis=0)

    def times(table, x):
        both = jnp.dot(table, jnp.concatenate(split(x), axis=0), preferred_element_type=f32)
        half = both.shape[0] // 2
        return both[:half] + both[half:]

    for l in range(3):
        wide = jnp.dot(couplings[l], spread, precision=HI, preferred_element_type=f32)
        tables[l] = stacked(jnp.dot(lift, jnp.where(same, wide, 0.0), precision=HI,
                                    preferred_element_type=f32))
        edges[l] = stacked(jnp.where(same, wide, 0.0)[:32, :32])

    def prepare(level, begin, end):
        def block(part, carry):
            for i in range(8):
                whole = packed[level, 8 * part + i].astype(f32)
                for tile in (0, 1):
                    stage[tile, 72 * i:72 * i + 64, :] = whole[:, 128 * tile:128 * tile + 128]
            rows = pl.ds(pl.multiple_of(8 * part, 8), 8)
            for at in range(64):
                for tile in (0, 1):
                    inv[level, at, tile, rows, :] = stage[tile, pl.ds(at, 8, 72), :]
            return carry

        lax.fori_loop(begin, end, block, 0)

    nb = neighbours[...]
    picks[...] = jnp.where(nb < 256, nb, 512)

    loads[0].wait()
    prepare(0, 0, 8)
    loads[1].wait()
    loads[2].wait()

    pl.semaphore_wait(
        barrier,
        5 + (d > 0).astype(jnp.int32) + (d < tm_size - 1).astype(jnp.int32)
        + (m > 0).astype(jnp.int32) + (m < groups - 1).astype(jnp.int32))

    lists = [
        pltpu.make_async_remote_copy(slots.at[0], slots.at[1], slot_send.at[0], slot_recv.at[0],
                                     device_id=(d, above), device_id_type=MESH),
        pltpu.make_async_remote_copy(slots.at[0], slots.at[2], slot_send.at[1], slot_recv.at[1],
                                     device_id=(d, below), device_id_type=MESH)]
    for copy in lists:
        copy.start()

    back = jnp.maximum(d - 1, 0)
    forth = jnp.where(d > 0, d - 1, 1)
    ahead = pltpu.make_async_remote_copy(source.at[0], next_source, src_send, src_recv,
                                         device_id=(forth, k), device_id_type=MESH)

    @pl.when(d > 0)
    def _():
        ahead.start()

    @pl.when(d == tm_size - 1)
    def _():
        next_source[...] = jnp.zeros_like(next_source)

    for copy in lists:
        copy.wait()
    for row, (held, line, begin, exists) in enumerate(
            [(1, 1, 256, k > 0), (2, 0, 272, k < space_size - 1)]):
        for tile in (0, 1):
            lanes = pl.ds(128 * tile, 128)
            entry = jnp.broadcast_to(neighbours[row:row + 1, lanes], (8, 128)) - begin
            listed = jnp.broadcast_to(slots[held, line:line + 1, :], (8, 128))
            taken = lane_take(listed, jnp.clip(entry, 0, 15))
            limit = jnp.where(exists, 16, 0)
            valid = (entry >= 0) & (entry < limit)
            where_halo[row, :, lanes] = jnp.where(valid, taken, 512)

    def take_from(block, index_of):
        halves = []
        for tile in (0, 1):
            index = index_of(tile)
            spot = index & 127
            part = index >> 7
            halves.append(jnp.where(part == 0, lane_take(block[:, :128], spot),
                                    jnp.where(part == 1, lane_take(block[:, 128:], spot), 0.0)))
        return jnp.concatenate(halves, axis=1)

    def across(ref, begin, size, stride=None):
        return jnp.concatenate([ref[tile, pl.ds(begin, size, stride), :] for tile in (0, 1)], axis=1)

    def phi(level, slot, value, meanwhile=None):
        for tile in (0, 1):
            state[tile] = value[:, 128 * tile:128 * tile + 128]
        traces[slot, 0] = across(state, 0, 16, 4)
        traces[slot, 1] = across(state, 3, 16, 4)
        moves = [
            pltpu.make_async_remote_copy(traces.at[slot, 1], halo.at[slot, 0], halo_send.at[slot, 0],
                                         halo_recv.at[slot, 0], device_id=(d, above),
                                         device_id_type=MESH),
            pltpu.make_async_remote_copy(traces.at[slot, 0], halo.at[slot, 1], halo_send.at[slot, 1],
                                         halo_recv.at[slot, 1], device_id=(d, below),
                                         device_id_type=MESH)]
        for move in moves:
            move.start()
        faces = [
            traces[slot, 0], traces[slot, 1],
            jnp.concatenate([value[16 * q:16 * q + 4, :] for q in range(4)], axis=0),
            jnp.concatenate([value[16 * q + 12:16 * q + 16, :] for q in range(4)], axis=0),
            value[0:16, :], value[48:64, :]]
        picked = jnp.concatenate(
            [take_from(faces[f ^ 1], lambda tile, f=f: jnp.broadcast_to(
                picks[f:f + 1, 128 * tile:128 * tile + 128], (16, 128))) for f in range(6)], axis=0)
        coupled = times(tables[level], picked)
        known = mass[...] * value - coupled
        for tile in (0, 1):
            rhs[tile] = known[:, 128 * tile:128 * tile + 128]

        def early(q, total):
            for step in (1, 2):
                at = 4 * q + step
                total = total + inv[level, at] * rhs[:, pl.ds(at, 1), :]
            return total

        total = lax.fori_loop(0, 16, early, jnp.zeros((2, 64, 128), f32), unroll=2)
        if meanwhile is not None:
            prepare(*meanwhile)
        for move in moves:
            move.wait()
        got = jnp.concatenate(
            [take_from(halo[slot, row], lambda tile, row=row: jnp.concatenate(
                [where_halo[row, :, 128 * tile:128 * tile + 128]] * 2, axis=0))
             for row in (0, 1)], axis=0)
        change = times(edges[level], got)
        for row, kept, first in ((0, low, 0), (1, high, 3)):
            for tile in (0, 1):
                kept[tile] = (rhs[tile, pl.ds(first, 16, 4), :]
                              - change[16 * row:16 * row + 16, 128 * tile:128 * tile + 128])

        def late(q, total):
            total = total + inv[level, 4 * q] * low[:, pl.ds(q, 1), :]
            return total + inv[level, 4 * q + 3] * high[:, pl.ds(q, 1), :]

        total = lax.fori_loop(0, 16, late, total, unroll=2)
        return jnp.concatenate([total[0], total[1]], axis=1)

    value = source[1]
    value = phi(0, 0, value, (1, 0, 3)) + source[2]
    value = phi(0, 1, value, (1, 3, 6)) + source[3]
    value = phi(0, 0, value, (1, 6, 8))

    @pl.when(d < tm_size - 1)
    def _():
        ahead.wait_recv()

    @pl.when(d > 0)
    def _():
        ahead.wait_send()

    r_all[j] = value + next_source[...]
    shares = [pltpu.make_async_remote_copy(r_all.at[j], r_all.at[j], r_send.at[i], r_recv.at[j],
                                           device_id=(peer, k), device_id_type=MESH)
              for i, peer in enumerate(peers)]
    for share in shares:
        share.start()

    def share_arrived(i):
        @pl.when(j != i)
        def _():
            pltpu.make_async_remote_copy(r_all.at[i], r_all.at[i], r_send.at[0], r_recv.at[i],
                                         device_id=(peers[0], k), device_id_type=MESH).wait_recv()

    prepare(2, 0, 8)
    first = phi(2, 1, initial[...])
    share_arrived(0)
    value = phi(1, 0, r_all[0])
    share_arrived(1)
    value = phi(1, 1, value + r_all[1])
    share_arrived(2)
    value = phi(1, 0, value + r_all[2])
    share_arrived(3)
    w_out[...] = value + r_all[3]
    for share in shares:
        share.wait_send()

    onward = pltpu.make_async_remote_copy(w_out, w_in, w_send, w_recv,
                                          device_id=(jnp.where(m < groups - 1, d + 4, d - 4), k),
                                          device_id_type=MESH)

    @pl.when(m == 0)
    def _():
        w_in[...] = initial[...]
        w_out[...] = w_out[...] + first

    @pl.when(m > 0)
    def _():
        onward.wait_recv()

    @pl.when((m > 0) & (m < groups - 1))
    def _():
        w_out[...] = w_out[...] + phi(2, 2, w_in[...])

    @pl.when(m < groups - 1)
    def _():
        onward.start()

    value = w_in[...]
    for i in (1, 2, 3):
        moved = phi(1, i % 2, value) + r_all[i - 1]
        value = jnp.where(j >= i, moved, value)
    out[0] = value
    for i in (1, 2, 3):
        value = phi(0, (i + 1) % 2, value) + source[i]
        out[i] = value

    @pl.when(m < groups - 1)
    def _():
        onward.wait_send()


def local(tm_size, space_size, source, initial, mass, inverses, couplings, neighbours, sends):
    f32 = jnp.float32
    vmem = pl.BlockSpec(memory_space=pltpu.VMEM)
    dma = pltpu.SemaphoreType.DMA
    return pl.pallas_call(
        functools.partial(kernel, tm_size, space_size),
        out_shape=jax.ShapeDtypeStruct(source.shape, f32),
        in_specs=[vmem, vmem, vmem, pl.BlockSpec(memory_space=pl.ANY), vmem, vmem, vmem],
        out_specs=vmem,
        scratch_shapes=[
            pltpu.VMEM(inverses.shape, jnp.bfloat16),
            pltpu.VMEM((2, 576, 128), f32),
            pltpu.VMEM((3, 64, 2, 64, 128), f32),
            pltpu.VMEM((3, 128, 192), jnp.bfloat16),
            pltpu.VMEM((3, 64, 64), jnp.bfloat16),
            pltpu.VMEM((2, 64, 128), f32),
            pltpu.VMEM((3, 2, 16, 256), f32),
            pltpu.VMEM((3, 2, 16, 256), f32),
            pltpu.VMEM((2, 64, 128), f32),
            pltpu.VMEM((2, 16, 128), f32),
            pltpu.VMEM((2, 16, 128), f32),
            pltpu.VMEM((3, 8, 128), jnp.int32),
            pltpu.VMEM((6, 256), jnp.int32),
            pltpu.VMEM((2, 8, 256), jnp.int32),
            pltpu.VMEM((64, 256), f32),
            pltpu.VMEM((4, 64, 256), f32),
            pltpu.VMEM((64, 256), f32),
            pltpu.VMEM((64, 256), f32),
            dma((3,)), dma((3, 2)), dma((3, 2)), dma((2,)), dma((2,)), dma, dma,
            dma((3,)), dma((4,)), dma, dma,
        ],
        compiler_params=pltpu.CompilerParams(collective_id=0, has_side_effects=True),
        name="cycle",
    )(source, initial, mass, inverses, couplings.reshape(3, 96, 16), neighbours, sends)


def solution(mesh):
    placed = (
        P("tm", None, "space"),
        P(None, "space"),
        P(None, "space"),
        P(None, None, None, "space"),
        P(),
        P(None, "space"),
        P(None, "space"),
    )
    return jax.shard_map(
        functools.partial(local, mesh.shape["tm"], mesh.shape["space"]),
        mesh=mesh, in_specs=placed, out_specs=P("tm", None, "space"), check_vma=False)
```

```python
import functools
import jax
import jax.numpy as jnp
from jax import lax
from jax.experimental import pallas as pl
from jax.experimental.pallas import tpu as pltpu
from jax.sharding import PartitionSpec as P

MESH = pl.DeviceIdType.MESH
HI = lax.Precision.HIGHEST


def lane_take(block, index):
    return jnp.take_along_axis(block, index, axis=1, mode="promise_in_bounds")


def kernel(tm_size, space_size, source, initial, mass, inverses, couplings, neighbours, sends,
           out, packed, stage, inv, tables, edges, state, traces, halo, rhs, low, high, slots, picks, where_halo,
           next_source, r_all, w_in, s_all,
           inv_sem, halo_send, halo_recv, slot_send, slot_recv, src_send, src_recv,
           r_send, r_recv, s_send, s_recv):
    f32 = jnp.float32
    d = lax.axis_index("tm")
    k = lax.axis_index("space")
    j = lax.rem(d, 4)
    m = lax.div(d, 4)
    groups = tm_size // 4
    above = lax.rem(k + 1, space_size)
    below = lax.rem(k + space_size - 1, space_size)
    peers = [4 * m + lax.rem(j + step, 4) for step in (1, 2, 3)]

    loads = [pltpu.make_async_copy(inverses.at[l], packed.at[l], inv_sem.at[l]) for l in range(3)]
    loads[0].start()
    loads[1].start()
    loads[2].start()

    barrier = pltpu.get_barrier_semaphore()

    def greet(t, s):
        pl.semaphore_signal(barrier, inc=1, device_id=(t, s), device_id_type=MESH)

    greet(d, above)
    greet(d, below)
    for peer in peers:
        greet(peer, k)

    @pl.when(d > 0)
    def _():
        greet(d - 1, k)

    @pl.when(d < tm_size - 1)
    def _():
        greet(d + 1, k)

    for t in range(groups):
        @pl.when(m != t)
        def _(t=t):
            greet(4 * t + j, k)

    slots[0] = jnp.zeros((8, 128), jnp.int32)
    slots[0, 0:2, 0:16] = sends[...]

    n = lax.broadcasted_iota(jnp.int32, (64, 96), 0)
    col = lax.broadcasted_iota(jnp.int32, (64, 96), 1)
    a, b, c = n & 3, (n >> 2) & 3, n >> 4
    face, point = col >> 4, col & 15
    axis = face >> 1
    fixed = jnp.where(axis == 0, a, jnp.where(axis == 1, b, c))
    place = jnp.where(axis == 0, b + 4 * c, jnp.where(axis == 1, a + 4 * c, a + 4 * b))
    lift = ((fixed == 3 * (face & 1)) & (place == point)).astype(f32)
    spread = (lax.broadcasted_iota(jnp.int32, (16, 96), 0)
              == (lax.broadcasted_iota(jnp.int32, (16, 96), 1) & 15)).astype(f32)
    same = (lax.broadcasted_iota(jnp.int32, (96, 96), 0) >> 4
            == lax.broadcasted_iota(jnp.int32, (96, 96), 1) >> 4)
    def split(x):
        top = x.astype(jnp.bfloat16)
        return top, (x - top.astype(f32)).astype(jnp.bfloat16)

    def stacked(x):
        top, rest = split(x)
        return jnp.concatenate([jnp.concatenate([top, top], axis=1),
                                jnp.concatenate([rest, rest], axis=1)], axis=0)

    def times(table, x):
        both = jnp.dot(table, jnp.concatenate(split(x), axis=0), preferred_element_type=f32)
        half = both.shape[0] // 2
        return both[:half] + both[half:]

    for l in range(3):
        wide = jnp.dot(couplings[l], spread, precision=HI, preferred_element_type=f32)
        tables[l] = stacked(jnp.dot(lift, jnp.where(same, wide, 0.0), precision=HI,
                                    preferred_element_type=f32))
        edges[l] = stacked(jnp.where(same, wide, 0.0)[:32, :32])

    def prepare(level, begin, end):
        def block(part, carry):
            for i in range(8):
                whole = packed[level, 8 * part + i].astype(f32)
                for tile in (0, 1):
                    stage[tile, 72 * i:72 * i + 64, :] = whole[:, 128 * tile:128 * tile + 128]
            rows = pl.ds(pl.multiple_of(8 * part, 8), 8)
            for at in range(64):
                for tile in (0, 1):
                    inv[level, at, tile, rows, :] = stage[tile, pl.ds(at, 8, 72), :]
            return carry

        lax.fori_loop(begin, end, block, 0)

    nb = neighbours[...]
    picks[...] = jnp.where(nb < 256, nb, 512)

    loads[0].wait()
    prepare(0, 0, 8)
    loads[1].wait()
    loads[2].wait()

    pl.semaphore_wait(
        barrier,
        4 + groups + (d > 0).astype(jnp.int32) + (d < tm_size - 1).astype(jnp.int32))

    lists = [
        pltpu.make_async_remote_copy(slots.at[0], slots.at[1], slot_send.at[0], slot_recv.at[0],
                                     device_id=(d, above), device_id_type=MESH),
        pltpu.make_async_remote_copy(slots.at[0], slots.at[2], slot_send.at[1], slot_recv.at[1],
                                     device_id=(d, below), device_id_type=MESH)]
    for copy in lists:
        copy.start()

    back = jnp.maximum(d - 1, 0)
    forth = jnp.where(d > 0, d - 1, 1)
    ahead = pltpu.make_async_remote_copy(source.at[0], next_source, src_send, src_recv,
                                         device_id=(forth, k), device_id_type=MESH)

    @pl.when(d > 0)
    def _():
        ahead.start()

    @pl.when(d == tm_size - 1)
    def _():
        next_source[...] = jnp.zeros_like(next_source)

    for copy in lists:
        copy.wait()
    for row, (held, line, begin, exists) in enumerate(
            [(1, 1, 256, k > 0), (2, 0, 272, k < space_size - 1)]):
        for tile in (0, 1):
            lanes = pl.ds(128 * tile, 128)
            entry = jnp.broadcast_to(neighbours[row:row + 1, lanes], (8, 128)) - begin
            listed = jnp.broadcast_to(slots[held, line:line + 1, :], (8, 128))
            taken = lane_take(listed, jnp.clip(entry, 0, 15))
            limit = jnp.where(exists, 16, 0)
            valid = (entry >= 0) & (entry < limit)
            where_halo[row, :, lanes] = jnp.where(valid, taken, 512)

    def take_from(block, index_of):
        halves = []
        for tile in (0, 1):
            index = index_of(tile)
            spot = index & 127
            part = index >> 7
            halves.append(jnp.where(part == 0, lane_take(block[:, :128], spot),
                                    jnp.where(part == 1, lane_take(block[:, 128:], spot), 0.0)))
        return jnp.concatenate(halves, axis=1)

    def across(ref, begin, size, stride=None):
        return jnp.concatenate([ref[tile, pl.ds(begin, size, stride), :] for tile in (0, 1)], axis=1)

    def phi(level, slot, value, meanwhile=None):
        for tile in (0, 1):
            state[tile] = value[:, 128 * tile:128 * tile + 128]
        traces[slot, 0] = across(state, 0, 16, 4)
        traces[slot, 1] = across(state, 3, 16, 4)
        moves = [
            pltpu.make_async_remote_copy(traces.at[slot, 1], halo.at[slot, 0], halo_send.at[slot, 0],
                                         halo_recv.at[slot, 0], device_id=(d, above),
                                         device_id_type=MESH),
            pltpu.make_async_remote_copy(traces.at[slot, 0], halo.at[slot, 1], halo_send.at[slot, 1],
                                         halo_recv.at[slot, 1], device_id=(d, below),
                                         device_id_type=MESH)]
        for move in moves:
            move.start()
        faces = [
            traces[slot, 0], traces[slot, 1],
            jnp.concatenate([value[16 * q:16 * q + 4, :] for q in range(4)], axis=0),
            jnp.concatenate([value[16 * q + 12:16 * q + 16, :] for q in range(4)], axis=0),
            value[0:16, :], value[48:64, :]]
        picked = jnp.concatenate(
            [take_from(faces[f ^ 1], lambda tile, f=f: jnp.broadcast_to(
                picks[f:f + 1, 128 * tile:128 * tile + 128], (16, 128))) for f in range(6)], axis=0)
        coupled = times(tables[level], picked)
        known = mass[...] * value - coupled
        for tile in (0, 1):
            rhs[tile] = known[:, 128 * tile:128 * tile + 128]

        def early(q, total):
            for step in (1, 2):
                at = 4 * q + step
                total = total + inv[level, at] * rhs[:, pl.ds(at, 1), :]
            return total

        total = lax.fori_loop(0, 16, early, jnp.zeros((2, 64, 128), f32), unroll=True)
        if meanwhile is not None:
            prepare(*meanwhile)
        for move in moves:
            move.wait()
        got = jnp.concatenate(
            [take_from(halo[slot, row], lambda tile, row=row: jnp.concatenate(
                [where_halo[row, :, 128 * tile:128 * tile + 128]] * 2, axis=0))
             for row in (0, 1)], axis=0)
        change = times(edges[level], got)
        for row, kept, first in ((0, low, 0), (1, high, 3)):
            for tile in (0, 1):
                kept[tile] = (rhs[tile, pl.ds(first, 16, 4), :]
                              - change[16 * row:16 * row + 16, 128 * tile:128 * tile + 128])

        def late(q, total):
            total = total + inv[level, 4 * q] * low[:, pl.ds(q, 1), :]
            return total + inv[level, 4 * q + 3] * high[:, pl.ds(q, 1), :]

        total = lax.fori_loop(0, 16, late, total, unroll=True)
        return jnp.concatenate([total[0], total[1]], axis=1)

    value = source[1]
    value = phi(0, 0, value, (1, 0, 3)) + source[2]
    value = phi(0, 1, value, (1, 3, 6)) + source[3]
    value = phi(0, 0, value, (1, 6, 8))

    @pl.when(d < tm_size - 1)
    def _():
        ahead.wait_recv()

    @pl.when(d > 0)
    def _():
        ahead.wait_send()

    r_all[j] = value + next_source[...]
    shares = [pltpu.make_async_remote_copy(r_all.at[j], r_all.at[j], r_send.at[i], r_recv.at[j],
                                           device_id=(peer, k), device_id_type=MESH)
              for i, peer in enumerate(peers)]
    for share in shares:
        share.start()

    def share_arrived(i):
        @pl.when(j != i)
        def _():
            pltpu.make_async_remote_copy(r_all.at[i], r_all.at[i], r_send.at[0], r_recv.at[i],
                                         device_id=(peers[0], k), device_id_type=MESH).wait_recv()

    prepare(2, 0, 8)
    first = phi(2, 1, initial[...])
    share_arrived(0)
    value = phi(1, 0, r_all[0])
    share_arrived(1)
    value = phi(1, 1, value + r_all[1])
    share_arrived(2)
    value = phi(1, 0, value + r_all[2])
    share_arrived(3)
    s_all[m] = value + r_all[3] + jnp.where(m == 0, first, 0.0)

    onward = {t: pltpu.make_async_remote_copy(
        s_all.at[m], s_all.at[m], s_send.at[t], s_recv.at[m],
        device_id=(jnp.where(m < t, 4 * t + j, lax.rem(d + 4, tm_size)), k), device_id_type=MESH)
        for t in range(groups - 1, 0, -1)}
    for t, copy in onward.items():
        @pl.when(m < t)
        def _(copy=copy):
            copy.start()

    for share in shares:
        share.wait_send()

    def s_arrived(i):
        pltpu.make_async_remote_copy(s_all.at[i], s_all.at[i], s_send.at[0], s_recv.at[i],
                                     device_id=(lax.rem(d + 4, tm_size), k),
                                     device_id_type=MESH).wait_recv()

    @pl.when(m == 0)
    def _():
        w_in[...] = initial[...]

    @pl.when(m > 0)
    def _():
        s_arrived(0)
        w_in[...] = s_all[0]

    def coarse(i, carry):
        moved = phi(2, 2 + lax.rem(i, 2), w_in[...])
        s_arrived(i)
        w_in[...] = moved + s_all[i]
        return carry

    lax.fori_loop(1, m, coarse, 0)

    value = w_in[...]
    for i in (1, 2, 3):
        moved = phi(1, i % 2, value) + r_all[i - 1]
        value = jnp.where(j >= i, moved, value)
    out[0] = value
    for i in (1, 2, 3):
        value = phi(0, (i + 1) % 2, value) + source[i]
        out[i] = value

    for t, copy in onward.items():
        @pl.when(m < t)
        def _(copy=copy):
            copy.wait_send()


def local(tm_size, space_size, source, initial, mass, inverses, couplings, neighbours, sends):
    f32 = jnp.float32
    vmem = pl.BlockSpec(memory_space=pltpu.VMEM)
    dma = pltpu.SemaphoreType.DMA
    return pl.pallas_call(
        functools.partial(kernel, tm_size, space_size),
        out_shape=jax.ShapeDtypeStruct(source.shape, f32),
        in_specs=[vmem, vmem, vmem, pl.BlockSpec(memory_space=pl.ANY), vmem, vmem, vmem],
        out_specs=vmem,
        scratch_shapes=[
            pltpu.VMEM(inverses.shape, jnp.bfloat16),
            pltpu.VMEM((2, 576, 128), f32),
            pltpu.VMEM((3, 64, 2, 64, 128), f32),
            pltpu.VMEM((3, 128, 192), jnp.bfloat16),
            pltpu.VMEM((3, 64, 64), jnp.bfloat16),
            pltpu.VMEM((2, 64, 128), f32),
            pltpu.VMEM((4, 2, 16, 256), f32),
            pltpu.VMEM((4, 2, 16, 256), f32),
            pltpu.VMEM((2, 64, 128), f32),
            pltpu.VMEM((2, 16, 128), f32),
            pltpu.VMEM((2, 16, 128), f32),
            pltpu.VMEM((3, 8, 128), jnp.int32),
            pltpu.VMEM((6, 256), jnp.int32),
            pltpu.VMEM((2, 8, 256), jnp.int32),
            pltpu.VMEM((64, 256), f32),
            pltpu.VMEM((4, 64, 256), f32),
            pltpu.VMEM((64, 256), f32),
            pltpu.VMEM((tm_size // 4, 64, 256), f32),
            dma((3,)), dma((4, 2)), dma((4, 2)), dma((2,)), dma((2,)), dma, dma,
            dma((3,)), dma((4,)), dma((tm_size // 4,)), dma((tm_size // 4,)),
        ],
        compiler_params=pltpu.CompilerParams(collective_id=0, has_side_effects=True),
        name="cycle",
    )(source, initial, mass, inverses, couplings.reshape(3, 96, 16), neighbours, sends)


def solution(mesh):
    placed = (
        P("tm", None, "space"),
        P(None, "space"),
        P(None, "space"),
        P(None, None, None, "space"),
        P(),
        P(None, "space"),
        P(None, "space"),
    )
    return jax.shard_map(
        functools.partial(local, mesh.shape["tm"], mesh.shape["space"]),
        mesh=mesh, in_specs=placed, out_specs=P("tm", None, "space"), check_vma=False)
```
